32 devices in a mesh: groups: 2 (over x), tm: 16 (over z, y, core).
Axes of the slice: x: 2, y: 2, z: 4, core: 2. Of those that a mesh axis runs over, the one named last changes fastest.
Arguments:
- pixels: bfloat16 [128, 128, 1536], P(('groups', 'tm')), parts along dimension 0, as said below
- prior_kv: bfloat16 [2, 16, 128, 640], P(None, 'groups'), parts along dimension 1, may hold values from -6 to 6
- w_embed: bfloat16 [1536, 1280], replicated, may hold values from -0.15625 to 0.15625
- ln_gain: float32 [1280], replicated, may hold values from 0.1 to 1.9
- w_query: bfloat16 [1280, 640], replicated, as said below
- w_key: bfloat16 [1280, 640], replicated, as said below
- w_value: bfloat16 [1280, 640], replicated, may hold values from -0.15625 to 0.15625
- w_out: bfloat16 [640, 1280], replicated, may hold values from -0.25 to 0.25
Outputs:
- encoded: bfloat16 [128, 128, 1280], P(('groups', 'tm')), parts along dimension 0
The draws below stay inside these ranges and needn't reach their ends.
There are 2 independent parts, one for each index of `groups`. The reference program is written for one: setup_inputs(seed, part) draws one part's arguments, and reference() takes and returns one part's arrays. A program takes and returns all parts, laid end to end along the dimension named above; an argument that names none is the same for every part. Nothing has to cross between parts.
Inputs may be any that keep to these rules, and one draw needn't show every extreme that they name: `pixels`: standardized pixel values. `w_query`: query projection, entries of order 1280 ** -0.5. `w_key`: key projection.
All inputs are finite; a program needn't handle non-finite values.
Results may differ from the reference program's by a relative error of at most 0.007.
Values may be sent and summed in bfloat16 or wider, within the bound.
A program may use at most 64 MiB of HBM per device.

```python
import math
import jax
import jax.numpy as jnp
from jax import lax

D = 1280
HEADS = 8
HEAD_DIM = 80
PIX = 1536
P_SIZE = 128
TUBELETS = 64
WINDOW = 8


def shared_matrix(key):
    return jax.random.truncated_normal(jax.random.fold_in(key, 11), -4.0, 4.0, (D, HEADS * HEAD_DIM), jnp.float32) * D ** (-0.5)


def draw_w_query(key, part):
    return shared_matrix(key).astype(jnp.bfloat16)


def draw_w_key(key, part):
    fresh = jax.random.truncated_normal(jax.random.fold_in(key, 31), -4.0, 4.0, (D, HEADS * HEAD_DIM), jnp.float32)
    return (fresh * D ** (-0.5)).astype(jnp.bfloat16)


def draw_pixels(key, part):
    shape = (TUBELETS, P_SIZE, PIX)
    return jax.random.truncated_normal(jax.random.fold_in(key, 53), -4.0, 4.0, shape, jnp.float32).astype(jnp.bfloat16)


def gaussian(stream_key, dims, scale, bound, kind=jnp.bfloat16):
    array = scale * jax.random.normal(stream_key, dims, jnp.float32)
    return jnp.clip(array, min=-bound, max=bound).astype(kind)


def setup_inputs(seed: int = 0, part: int = 0) -> dict:
    splits = jax.random.split(jax.random.key(seed), 9)
    part_keys = jax.random.split(jax.random.fold_in(splits[8], part), 9)
    return {
        "pixels": draw_pixels(jax.random.fold_in(jax.random.fold_in(splits[8], part), 71), part),
        "prior_kv": gaussian(part_keys[1], (2, WINDOW, P_SIZE, HEADS * HEAD_DIM), 1.0, 6.0),
        "w_embed": gaussian(splits[2], (PIX, D), PIX ** -0.5, 0.15625),
        "ln_gain": jnp.clip(1.0 + 0.18 * jax.random.normal(splits[3], (D,), jnp.float32), 0.1, 1.9),
        "w_query": draw_w_query(jax.random.fold_in(splits[8], 71), part),
        "w_key": draw_w_key(jax.random.fold_in(splits[8], 71), part),
        "w_value": gaussian(splits[6], (D, HEADS * HEAD_DIM), D ** -0.5, 0.15625),
        "w_out": gaussian(splits[7], (HEADS * HEAD_DIM, D), (HEADS * HEAD_DIM) ** -0.5, 0.25),
    }


def reference(pixels, prior_kv, w_embed, ln_gain, w_query, w_key, w_value, w_out):
    tub, pat, pix = pixels.shape
    flat = pixels.reshape(tub * pat, pix)
    embedded = jnp.dot(flat, w_embed, preferred_element_type=jnp.float32).astype(jnp.bfloat16)
    e_wide = embedded.astype(jnp.float32)
    center = e_wide - lax.optimization_barrier(jnp.mean(e_wide, axis=-1, keepdims=True))
    spread = lax.optimization_barrier(jnp.mean(center * center, axis=-1, keepdims=True))
    normed = (center * lax.rsqrt(spread + 1e-06) * ln_gain).astype(jnp.bfloat16)
    shape4 = (tub, pat, HEADS, HEAD_DIM)
    query = jnp.dot(normed, w_query, preferred_element_type=jnp.float32).astype(jnp.bfloat16).reshape(shape4)
    key = jnp.dot(normed, w_key, preferred_element_type=jnp.float32).astype(jnp.bfloat16).reshape(shape4)
    value = jnp.dot(normed, w_value, preferred_element_type=jnp.float32).astype(jnp.bfloat16).reshape(shape4)
    scale = 1.0 / math.sqrt(HEAD_DIM)
    prior_key = prior_kv[0].reshape(WINDOW, pat, HEADS, HEAD_DIM)
    prior_value = prior_kv[1].reshape(WINDOW, pat, HEADS, HEAD_DIM)
    key_pad = jnp.concatenate([prior_key, key], axis=0)
    value_pad = jnp.concatenate([prior_value, value], axis=0)
    query_wide = query.astype(jnp.float32)
    score_list = []
    for offset in range(WINDOW + 1):
        shifted = key_pad[WINDOW - offset:WINDOW - offset + tub].astype(jnp.float32)
        score_list.append(jnp.einsum('tphe,tphe->thp', query_wide, shifted) * scale)
    scores = jnp.stack(score_list, axis=0)
    top = lax.optimization_barrier(jnp.max(scores, axis=0, keepdims=True))
    expo = jnp.exp(scores - top)
    weights = (expo / lax.optimization_barrier(jnp.sum(expo, axis=0, keepdims=True))).astype(jnp.bfloat16)
    mixed = jnp.zeros((tub, pat, HEADS, HEAD_DIM), jnp.float32)
    for offset in range(WINDOW + 1):
        shifted = value_pad[WINDOW - offset:WINDOW - offset + tub].astype(jnp.float32)
        mixed = mixed + jnp.einsum('thp,tphe->tphe', weights[offset].astype(jnp.float32), shifted)
    mixed = mixed.astype(jnp.bfloat16).reshape(tub * pat, HEADS * HEAD_DIM)
    encoded = e_wide + jnp.dot(mixed, w_out, preferred_element_type=jnp.float32)
    return encoded.astype(jnp.bfloat16).reshape(tub, pat, D)
```

```python
import math

import jax
import jax.numpy as jnp
from jax import lax
from jax.experimental import pallas as pl
from jax.experimental.pallas import tpu as pltpu
from jax.sharding import PartitionSpec as P

HEADS = 8
HEAD_DIM = 80
LANE = 128
TILE = 16
SUB = 8
QUAD = 4
MESH = pl.DeviceIdType.MESH


def kernel(
    pixels,
    prior,
    w_embed,
    ln_gain,
    w_query,
    w_key,
    w_value,
    w_out,
    encoded,
    pix,
    old,
    we,
    gain,
    wq,
    wk,
    wv,
    wo,
    emb,
    out_norm,
    nrm,
    qry,
    kv,
    mixed_out,
    mixed_in,
    bias,
    w_sem,
    pix_sem,
    old_sem,
    norm_send,
    norm_recv,
    halo_send,
    halo_recv,
    mix_send,
    mix_recv,
):
    count = lax.axis_size("tm")
    me = lax.axis_index("tm")
    tub, patches, _ = pixels.shape
    width = w_embed.shape[1]
    half = w_key.shape[1]
    block = patches // QUAD
    chunks = block // SUB
    rows = tub * SUB
    side_rows = 2 * rows
    r = lax.rem(me, QUAD)
    first = me - r
    side = r // 2
    peers = [r, r + 1 - 2 * lax.rem(r, 2), lax.rem(r + 2, QUAD), QUAD - 1 - r]
    has_before = me >= QUAD
    has_after = me + QUAD < count
    low_side = side == 0
    high_side = side == 1

    def aligned(value, size):
        return pl.ds(pl.multiple_of(value, size), size)

    def step_of(k, own):
        return k + 1 if own else 3 * k

    def load_pix(t, g):
        own = t in (1, 2)
        source = peers[g if own else 2 + g] * block + (t // 2) * TILE
        return pltpu.make_async_copy(
            pixels.at[:, aligned(source, TILE), :], pix.at[t, g], pix_sem.at[t, g]
        )

    def wait_pix(t, g):
        pltpu.make_async_copy(
            pixels.at[:, pl.ds(0, TILE), :], pix.at[t, g], pix_sem.at[t, g]
        ).wait()

    def load_weight(source, target, index):
        return pltpu.make_async_copy(source, target, w_sem.at[index])

    get_we = load_weight(w_embed, we, 0)
    get_gain = load_weight(ln_gain, gain, 1)
    get_wk = load_weight(w_key, wk, 2)
    get_wv = load_weight(w_value, wv, 3)
    get_wq = load_weight(w_query, wq, 4)
    get_wo = load_weight(w_out, wo, 5)
    get_old = pltpu.make_async_copy(
        prior.at[:, :, aligned(r * block, block), :], old, old_sem.at[0]
    )

    def send_norm(d, c):
        k, h = c // 2, lax.rem(c, 2)
        t, g = (k + 1, 1) if d == 1 else (3 * k, d - 2)
        return pltpu.make_async_remote_copy(
            src_ref=out_norm.at[t, g, h],
            dst_ref=nrm.at[c, aligned(r * rows, rows)],
            send_sem=norm_send.at[d, c],
            recv_sem=norm_recv.at[d, c],
            device_id={"tm": first + peers[d]},
            device_id_type=MESH,
        )

    def send_halo(c):
        return pltpu.make_async_remote_copy(
            src_ref=kv.at[c, pl.ds(2 * side_rows, side_rows)],
            dst_ref=kv.at[c, pl.ds(0, side_rows)],
            send_sem=halo_send.at[c],
            recv_sem=halo_recv.at[c],
            device_id={"tm": me + QUAD},
            device_id_type=MESH,
        )

    def send_mix(d, c):
        return pltpu.make_async_remote_copy(
            src_ref=mixed_out.at[c, aligned(peers[d] * rows, rows)],
            dst_ref=mixed_in.at[d, c],
            send_sem=mix_send.at[d, c],
            recv_sem=mix_recv.at[d, c],
            device_id={"tm": first + peers[d]},
            device_id_type=MESH,
        )

    barrier = pltpu.get_barrier_semaphore()
    for d in range(1, QUAD):
        pl.semaphore_signal(
            barrier, inc=1, device_id={"tm": first + peers[d]}, device_id_type=MESH
        )

    @pl.when(has_before)
    def _():
        pl.semaphore_signal(barrier, inc=1, device_id={"tm": me - QUAD}, device_id_type=MESH)

    @pl.when(has_after)
    def _():
        pl.semaphore_signal(barrier, inc=1, device_id={"tm": me + QUAD}, device_id_type=MESH)

    load_pix(0, 0).start()
    load_pix(0, 1).start()
    get_we.start()
    get_gain.start()
    for t in range(1, 4):
        for g in range(2):
            load_pix(t, g).start()
    get_wk.start()
    get_wv.start()
    get_wq.start()

    @pl.when(me < QUAD)
    def _():
        get_old.start()

    get_wo.start()

    row = lax.broadcasted_iota(jnp.int32, (2 * side_rows, 2 * side_rows), 0)
    col = lax.broadcasted_iota(jnp.int32, (2 * side_rows, 2 * side_rows), 1)
    at_t = lax.rem(row, side_rows) // SUB
    at_s = col // SUB
    seen = (lax.rem(row, SUB) == lax.rem(col, SUB)) & (at_s >= at_t) & (at_s <= at_t + 2 * tub)
    bias[...] = jnp.where(seen, 0.0, -jnp.inf)

    pl.semaphore_wait(
        barrier, QUAD - 1 + has_before.astype(jnp.int32) + has_after.astype(jnp.int32)
    )

    def project(normed, cs, row0, shape):
        for weight, lane in ((wk, 0), (wv, half)):
            part = jnp.dot(normed, weight[...], preferred_element_type=jnp.float32)
            kv[cs, aligned(side_rows + row0, side_rows), pl.ds(lane, half)] = part.astype(
                jnp.bfloat16
            ).reshape(shape)
        query = jnp.dot(normed, wq[...], preferred_element_type=jnp.float32)
        qry[cs, aligned(row0, side_rows), :] = query.astype(jnp.bfloat16).reshape(shape)

    def embed(t, carry):
        k = t // 2
        own = (t == 1) | (t == 2)
        for g in range(2):
            wait_pix(t, g)

        @pl.when(t == 0)
        def _():
            get_we.wait()
            get_gain.wait()

        flat = pix[t].reshape(2 * tub * TILE, pix.shape[4])
        embedded = jnp.dot(flat, we[...], preferred_element_type=jnp.float32).astype(jnp.bfloat16)
        emb[t] = embedded.reshape(2, tub, TILE, width)
        wide = embedded.astype(jnp.float32)
        center = wide - jnp.mean(wide, axis=-1, keepdims=True)
        spread = jnp.mean(center * center, axis=-1, keepdims=True)
        scaled = center * lax.rsqrt(spread + 1e-06) * gain[...].reshape(1, width)
        scaled = scaled.reshape(2, tub, TILE, width)
        for g in range(2):
            for h in range(2):
                piece = scaled[g, :, h * SUB : (h + 1) * SUB, :].reshape(rows, width)
                out_norm[t, g, h] = piece.astype(jnp.bfloat16)

        @pl.when(own)
        def _():
            for h in range(2):
                send_norm(1, 2 * k + h).start()
                nrm[2 * k + h, aligned(r * rows, rows), :] = out_norm[t, 0, h]

        @pl.when(jnp.logical_not(own))
        def _():
            for h in range(2):
                for d in (2, 3):
                    send_norm(d, 2 * k + h).start()

        @pl.when(t >= 2)
        def _():
            j = t - 2

            @pl.when(t == 2)
            def _():
                get_wk.wait()
                get_wv.wait()
                get_wq.wait()

            for h in range(2):
                send_norm(1, 2 * j + h).wait_recv()
            cs = pl.ds(2 * j, 2)
            normed = nrm[cs, aligned(side * side_rows, side_rows), :]
            project(
                normed.reshape(2 * side_rows, width),
                cs,
                side * side_rows,
                (2, side_rows, half),
            )

            @pl.when(high_side & has_after)
            def _():
                for h in range(2):
                    send_halo(2 * j + h).start()

        return carry

    lax.fori_loop(0, 4, embed, 0)

    @pl.when(me < QUAD)
    def _():
        get_old.wait()
        for which in range(2):
            for k in range(chunks // 2):
                wide = old[which, :, k * TILE : (k + 1) * TILE, :].astype(jnp.float32)
                for h in range(2):
                    piece = wide[:, h * SUB : (h + 1) * SUB, :].reshape(side_rows, half)
                    kv[2 * k + h, pl.ds(0, side_rows), pl.ds(which * half, half)] = piece.astype(
                        jnp.bfloat16
                    )

    scale = 1.0 / math.sqrt(HEAD_DIM)
    window = 2 * LANE
    lane = lax.broadcasted_iota(jnp.int32, (1, window), 1)

    def attend(jobs):
        stages = []
        for c, which in jobs:
            start = which * side_rows
            for pair in range(HEADS // 2):
                low = 2 * pair * HEAD_DIM
                base = low // LANE * LANE
                begins = [low + head * HEAD_DIM - base for head in range(2)]
                pick = [(lane >= begin) & (lane < begin + HEAD_DIM) for begin in begins]
                q = qry[c, aligned(start, side_rows), pl.ds(base, window)]
                both = jnp.concatenate(
                    [q * jnp.where(one, 1.0, 0.0).astype(jnp.bfloat16) for one in pick], axis=0
                )
                keys = kv[c, pl.ds(pl.multiple_of(start, side_rows), 2 * side_rows), pl.ds(base, window)]
                found = lax.dot_general(
                    both, keys, (((1,), (1,)), ((), ())), preferred_element_type=jnp.float32
                )
                stages.append((c, start, base, pick, found))
        weights = []
        for c, start, base, pick, found in stages:
            score = found * scale + bias[...]
            top = jnp.max(score, axis=-1, keepdims=True)
            expo = jnp.exp(score - top)
            total = jnp.sum(expo, axis=-1, keepdims=True)
            weights.append((expo * (1.0 / total)).astype(jnp.bfloat16))
        tiles = None
        for index, (c, start, base, pick, found) in enumerate(stages):
            if index % (HEADS // 2) == 0:
                tiles = [None] * (half // LANE)
            values = kv[
                c, pl.ds(pl.multiple_of(start, side_rows), 2 * side_rows), pl.ds(half + base, window)
            ]
            blend = jnp.dot(weights[index], values, preferred_element_type=jnp.float32)
            part = jnp.where(pick[0], blend[:side_rows], 0.0) + jnp.where(
                pick[1], blend[side_rows:], 0.0
            )
            for half_window in range(2):
                piece = part[:, half_window * LANE : (half_window + 1) * LANE]
                at = base // LANE + half_window
                tiles[at] = piece if tiles[at] is None else tiles[at] + piece
            if index % (HEADS // 2) == HEADS // 2 - 1:
                mixed = jnp.concatenate(tiles, axis=1).astype(jnp.bfloat16)
                mixed_out[c, aligned(start, side_rows), :] = mixed

    def give_far(c):
        for d in (2, 3):
            send_mix(d, c).start()

    def give_near(c):
        send_mix(1, c).start()
        mixed_in[0, c] = mixed_out[c, aligned(r * rows, rows), :]

    def arrive(c):
        for d in (2, 3):
            send_norm(d, c).wait_recv()
        row0 = (1 - side) * side_rows
        normed = nrm[c, aligned(row0, side_rows), :]
        project(normed, c, row0, (side_rows, half))

        @pl.when(low_side & has_after)
        def _():
            send_halo(c).start()

    arrive(0)

    @pl.when(high_side & has_before)
    def _():
        send_halo(0).wait_recv()

    attend([(0, 1 - side)])
    give_far(0)

    def chunk(c, carry):
        arrive(c)
        need = jnp.where(high_side, c, c - 1)

        @pl.when(has_before)
        def _():
            send_halo(need).wait_recv()

        attend([(c, 1 - side), (c - 1, side)])
        give_far(c)
        give_near(c - 1)
        return carry

    lax.fori_loop(1, chunks, chunk, 0)

    def finish(k, own):
        t = step_of(k, own)
        begin = 0 if own else 2
        taken = mixed_in[pl.ds(begin, 2), pl.ds(2 * k, 2)].reshape(2 * tub * TILE, half)
        result = jnp.dot(taken, wo[...], preferred_element_type=jnp.float32)
        result = result.reshape(2, 2, tub, SUB, width)
        for g in range(2):
            whole = jnp.concatenate([result[g, 0], result[g, 1]], axis=1)
            whole = whole + emb[t, g].astype(jnp.float32)
            target = peers[begin + g] * block + k * TILE
            encoded[:, aligned(target, TILE), :] = whole.astype(jnp.bfloat16)

    get_wo.wait()
    for c in range(2):
        send_mix(1, c).wait_recv()
    finish(0, True)

    @pl.when(low_side & has_before)
    def _():
        send_halo(chunks - 1).wait_recv()

    attend([(chunks - 1, side)])
    give_near(chunks - 1)

    for c in range(2):
        for d in (2, 3):
            send_mix(d, c).wait_recv()
    finish(0, False)
    for c in range(2, 4):
        send_mix(1, c).wait_recv()
    finish(1, True)
    for c in range(2, 4):
        for d in (2, 3):
            send_mix(d, c).wait_recv()
    finish(1, False)

    def drain(c, carry):
        for d in range(1, QUAD):
            send_norm(d, c).wait_send()
            send_mix(d, c).wait_send()

        @pl.when(has_after)
        def _():
            send_halo(c).wait_send()

        return carry

    lax.fori_loop(0, chunks, drain, 0)


def body(pixels, prior_kv, w_embed, ln_gain, w_query, w_key, w_value, w_out):
    tub, pat, pix = pixels.shape
    width = w_embed.shape[1]
    half = w_key.shape[1]
    block = pat // QUAD
    chunks = block // SUB
    rows = tub * SUB
    bf16 = jnp.bfloat16
    dma = pltpu.SemaphoreType.DMA
    return pl.pallas_call(
        kernel,
        out_shape=pltpu.VMEM((tub, pat, width), bf16),
        in_specs=[pl.BlockSpec(memory_space=pl.ANY)] * 8,
        out_specs=pl.BlockSpec(memory_space=pltpu.VMEM),
        scratch_shapes=[
            pltpu.VMEM((4, 2, tub, TILE, pix), bf16),
            pltpu.VMEM((2, 2 * tub, block, half), bf16),
            pltpu.VMEM(w_embed.shape, bf16),
            pltpu.VMEM((width,), jnp.float32),
            pltpu.VMEM(w_query.shape, bf16),
            pltpu.VMEM(w_key.shape, bf16),
            pltpu.VMEM(w_value.shape, bf16),
            pltpu.VMEM(w_out.shape, bf16),
            pltpu.VMEM((4, 2, tub, TILE, width), bf16),
            pltpu.VMEM((4, 2, 2, rows, width), bf16),
            pltpu.VMEM((chunks, QUAD * rows, width), bf16),
            pltpu.VMEM((chunks, QUAD * rows, half), bf16),
            pltpu.VMEM((chunks, 6 * rows, 2 * half), bf16),
            pltpu.VMEM((chunks, QUAD * rows, half), bf16),
            pltpu.VMEM((QUAD, chunks, rows, half), bf16),
            pltpu.VMEM((QUAD * rows, QUAD * rows), jnp.float32),
            dma((6,)),
            dma((4, 2)),
            dma((1,)),
            dma((QUAD, chunks)),
            dma((QUAD, chunks)),
            dma((chunks,)),
            dma((chunks,)),
            dma((QUAD, chunks)),
            dma((QUAD, chunks)),
        ],
        compiler_params=pltpu.CompilerParams(
            collective_id=0, has_side_effects=True, vmem_limit_bytes=60000000
        ),
    )(pixels, prior_kv, w_embed, ln_gain, w_query, w_key, w_value, w_out)


def solution(mesh):
    placed = (
        P(("groups", "tm"), None, None),
        P(None, "groups", None, None),
        P(),
        P(),
        P(),
        P(),
        P(),
        P(),
    )
    return jax.shard_map(
        body, mesh=mesh, in_specs=placed, out_specs=P(("groups", "tm"), None, None), check_vma=False
    )
```

```python
import math

import jax
import jax.numpy as jnp
from jax import lax
from jax.experimental import pallas as pl
from jax.experimental.pallas import tpu as pltpu
from jax.sharding import PartitionSpec as P

HEADS = 8
HEAD_DIM = 80
LANE = 128
TILE = 16
SUB = 8
RAW = 2
QUAD = 4
MESH = pl.DeviceIdType.MESH


def kernel(
    pixels,
    prior,
    w_embed,
    ln_gain,
    w_query,
    w_key,
    w_value,
    w_out,
    encoded,
    pix,
    raw,
    old,
    we,
    gain,
    wq,
    wk,
    wv,
    wo,
    emb,
    out_norm,
    nrm,
    halo,
    qry,
    kv,
    mixed_out,
    mixed_in,
    bias,
    w_sem,
    pix_sem,
    old_sem,
    raw_sem,
    norm_send,
    norm_recv,
    halo_send,
    halo_recv,
    mix_send,
    mix_recv,
):
    count = lax.axis_size("tm")
    me = lax.axis_index("tm")
    tub, patches, _ = pixels.shape
    width = w_embed.shape[1]
    half = w_key.shape[1]
    block = patches // QUAD
    chunks = block // SUB
    rows = tub * SUB
    side_rows = 2 * rows
    r = lax.rem(me, QUAD)
    first = me - r
    side = r // 2
    peers = [r, r + 1 - 2 * lax.rem(r, 2), lax.rem(r + 2, QUAD), QUAD - 1 - r]
    has_before = me >= QUAD
    has_after = me + QUAD < count
    low_side = side == 0
    in_first = me < QUAD
    high_side = side == 1

    def aligned(value, size):
        return pl.ds(pl.multiple_of(value, size), size)

    def step_of(k, own):
        return k + 1 if own else 3 * k

    def load_pix(t, g):
        own = t in (1, 2)
        source = peers[g if own else 2 + g] * block + (t // 2) * TILE
        return pltpu.make_async_copy(
            pixels.at[:, aligned(source, TILE), :], pix.at[t, g], pix_sem.at[t, g]
        )

    def wait_pix(t, g):
        pltpu.make_async_copy(
            pixels.at[:, pl.ds(0, TILE), :], pix.at[t, g], pix_sem.at[t, g]
        ).wait()

    def load_weight(source, target, index):
        return pltpu.make_async_copy(source, target, w_sem.at[index])

    get_we = load_weight(w_embed, we, 0)
    get_gain = load_weight(ln_gain, gain, 1)
    get_wk = load_weight(w_key, wk, 2)
    get_wv = load_weight(w_value, wv, 3)
    get_wq = load_weight(w_query, wq, 4)
    get_wo = load_weight(w_out, wo, 5)
    get_old = pltpu.make_async_copy(
        prior.at[:, :, aligned(r * block, block), :], old, old_sem.at[0]
    )

    def send_norm(d, c):
        k, h = c // 2, lax.rem(c, 2)
        t, g = (k + 1, 1) if d == 1 else (3 * k, d - 2)
        return pltpu.make_async_remote_copy(
            src_ref=out_norm.at[t, g, h],
            dst_ref=nrm.at[c, aligned(r * rows, rows)],
            send_sem=norm_send.at[d, c],
            recv_sem=norm_recv.at[d, c],
            device_id={"tm": first + peers[d]},
            device_id_type=MESH,
        )

    def send_raw():
        return pltpu.make_async_remote_copy(
            src_ref=pixels.at[pl.ds(0, RAW), aligned(peers[2] * block, TILE), :],
            dst_ref=raw,
            send_sem=raw_sem.at[0],
            recv_sem=raw_sem.at[1],
            device_id={"tm": first + peers[2]},
            device_id_type=MESH,
        )

    def send_rest(c):
        skip = RAW * SUB
        return pltpu.make_async_remote_copy(
            src_ref=out_norm.at[0, 0, c, pl.ds(skip, rows - skip)],
            dst_ref=nrm.at[c, pl.ds(pl.multiple_of(r * rows + skip, TILE), rows - skip)],
            send_sem=norm_send.at[2, c],
            recv_sem=norm_recv.at[2, c],
            device_id={"tm": first + peers[2]},
            device_id_type=MESH,
        )

    def halo_copy(source, g, c, j, target):
        return pltpu.make_async_remote_copy(
            src_ref=source,
            dst_ref=halo.at[c, aligned(j * rows, rows)],
            send_sem=halo_send.at[g, c],
            recv_sem=halo_recv.at[j, c],
            device_id={"tm": target},
            device_id_type=MESH,
        )

    def give_halo(t, g, h):
        c = 2 * (t // 2) + h
        return halo_copy(out_norm.at[t, g, h], g, c, lax.rem(r, 2), first + QUAD + peers[g])

    def forward_halo(d, c):
        source = nrm.at[c, aligned(peers[d] * rows, rows)]
        return halo_copy(source, d - 2, c, lax.rem(peers[d], 2), me + QUAD)

    def wait_halo(c):
        for j in range(2):
            halo_copy(nrm.at[c, pl.ds(0, rows)], 0, c, j, me + QUAD).wait_recv()

    def send_mix(d, c):
        return pltpu.make_async_remote_copy(
            src_ref=mixed_out.at[c, aligned(peers[d] * rows, rows)],
            dst_ref=mixed_in.at[d, c],
            send_sem=mix_send.at[d, c],
            recv_sem=mix_recv.at[d, c],
            device_id={"tm": first + peers[d]},
            device_id_type=MESH,
        )

    barrier = pltpu.get_barrier_semaphore()
    for d in range(1, QUAD):
        pl.semaphore_signal(
            barrier, inc=1, device_id={"tm": first + peers[d]}, device_id_type=MESH
        )

    def greet(target):
        pl.semaphore_signal(barrier, inc=1, device_id={"tm": target}, device_id_type=MESH)

    @pl.when(has_before)
    def _():
        greet(me - QUAD)

    @pl.when(has_after)
    def _():
        greet(me + QUAD)

    @pl.when(has_before & high_side)
    def _():
        greet(first - QUAD + peers[1])

    @pl.when(has_after & high_side)
    def _():
        greet(first + QUAD + peers[1])

    load_pix(0, 0).start()
    load_pix(0, 1).start()
    get_we.start()
    get_gain.start()

    def load_rest():
        for t in range(1, 4):
            for g in range(2):
                load_pix(t, g).start()
        get_wk.start()
        get_wv.start()
        get_wq.start()

        @pl.when(me < QUAD)
        def _():
            get_old.start()

        get_wo.start()

    row = lax.broadcasted_iota(jnp.int32, (2 * side_rows, 2 * side_rows), 0)
    col = lax.broadcasted_iota(jnp.int32, (2 * side_rows, 2 * side_rows), 1)
    at_t = lax.rem(row, side_rows) // SUB
    at_s = col // SUB
    seen = (lax.rem(row, SUB) == lax.rem(col, SUB)) & (at_s >= at_t) & (at_s <= at_t + 2 * tub)
    bias[...] = jnp.where(seen, 0.0, -jnp.inf)

    around = has_before.astype(jnp.int32) + has_after.astype(jnp.int32)
    pl.semaphore_wait(barrier, QUAD - 1 + around * (1 + side))

    @pl.when(in_first & high_side)
    def _():
        send_raw().start()

    def take(d, c):
        if d == 2:
            short = in_first & low_side & (c < 2)

            @pl.when(short)
            def _():
                send_rest(c).wait_recv()

            @pl.when(jnp.logical_not(short))
            def _():
                send_norm(2, c).wait_recv()

        else:
            send_norm(3, c).wait_recv()

        @pl.when(low_side & has_after)
        def _():
            forward_halo(d, c).start()

    def project(normed, cs, row0, shape):
        for weight, lane in ((wk, 0), (wv, half)):
            part = jnp.dot(normed, weight[...], preferred_element_type=jnp.float32)
            kv[cs, aligned(side_rows + row0, side_rows), pl.ds(lane, half)] = part.astype(
                jnp.bfloat16
            ).reshape(shape)
        query = jnp.dot(normed, wq[...], preferred_element_type=jnp.float32)
        qry[cs, aligned(row0, side_rows), :] = query.astype(jnp.bfloat16).reshape(shape)

    def normalize(flat):
        embedded = jnp.dot(flat, we[...], preferred_element_type=jnp.float32).astype(jnp.bfloat16)
        wide = embedded.astype(jnp.float32)
        center = wide - jnp.mean(wide, axis=-1, keepdims=True)
        spread = jnp.mean(center * center, axis=-1, keepdims=True)
        return embedded, center * lax.rsqrt(spread + 1e-06) * gain[...].reshape(1, width)

    def take_raw():
        send_raw().wait_recv()
        _, scaled = normalize(raw[...].reshape(RAW * TILE, pix.shape[4]))
        scaled = scaled.reshape(RAW, TILE, width)
        for h in range(2):
            piece = scaled[:, h * SUB : (h + 1) * SUB, :].reshape(RAW * SUB, width)
            start = pl.multiple_of(peers[2] * rows, rows)
            nrm[h, pl.ds(start, RAW * SUB), :] = piece.astype(jnp.bfloat16)

    def embed(t, carry):
        k = t // 2
        own = (t == 1) | (t == 2)
        for g in range(2):
            wait_pix(t, g)

        @pl.when(t == 0)
        def _():
            get_we.wait()
            get_gain.wait()
            load_rest()

        embedded, scaled = normalize(pix[t].reshape(2 * tub * TILE, pix.shape[4]))
        emb[t] = embedded.reshape(2, tub, TILE, width)
        scaled = scaled.reshape(2, tub, TILE, width)
        for g in range(2):
            for h in range(2):
                piece = scaled[g, :, h * SUB : (h + 1) * SUB, :].reshape(rows, width)
                out_norm[t, g, h] = piece.astype(jnp.bfloat16)

        @pl.when(own)
        def _():
            for h in range(2):
                send_norm(1, 2 * k + h).start()
                nrm[2 * k + h, aligned(r * rows, rows), :] = out_norm[t, 0, h]

            @pl.when(high_side & has_after)
            def _():
                for h in range(2):
                    for g in range(2):
                        give_halo(t, g, h).start()

        @pl.when(jnp.logical_not(own))
        def _():
            for h in range(2):
                short = in_first & high_side & (t == 0)

                @pl.when(short)
                def _():
                    send_rest(h).start()

                @pl.when(jnp.logical_not(short))
                def _():
                    send_norm(2, 2 * k + h).start()

                send_norm(3, 2 * k + h).start()

        @pl.when(t >= 2)
        def _():
            j = t - 2

            @pl.when(t == 2)
            def _():
                get_wk.wait()
                get_wv.wait()
                get_wq.wait()

            @pl.when((t == 3) & low_side)
            def _():
                @pl.when(in_first)
                def _():
                    take_raw()

                take(2, 0)

            for h in range(2):
                send_norm(1, 2 * j + h).wait_recv()
            cs = pl.ds(2 * j, 2)
            normed = nrm[cs, aligned(side * side_rows, side_rows), :]
            project(
                normed.reshape(2 * side_rows, width),
                cs,
                side * side_rows,
                (2, side_rows, half),
            )

        return carry

    lax.fori_loop(0, 4, embed, 0)

    @pl.when(me < QUAD)
    def _():
        get_old.wait()
        for which in range(2):
            for k in range(chunks // 2):
                wide = old[which, :, k * TILE : (k + 1) * TILE, :].astype(jnp.float32)
                for h in range(2):
                    piece = wide[:, h * SUB : (h + 1) * SUB, :].reshape(side_rows, half)
                    kv[2 * k + h, pl.ds(0, side_rows), pl.ds(which * half, half)] = piece.astype(
                        jnp.bfloat16
                    )

    scale = 1.0 / math.sqrt(HEAD_DIM)
    window = 2 * LANE
    lane = lax.broadcasted_iota(jnp.int32, (1, window), 1)

    def attend(jobs):
        stages = []
        for c, which in jobs:
            start = which * side_rows
            for pair in range(HEADS // 2):
                low = 2 * pair * HEAD_DIM
                base = low // LANE * LANE
                begins = [low + head * HEAD_DIM - base for head in range(2)]
                pick = [(lane >= begin) & (lane < begin + HEAD_DIM) for begin in begins]
                q = qry[c, aligned(start, side_rows), pl.ds(base, window)]
                both = jnp.concatenate(
                    [q * jnp.where(one, 1.0, 0.0).astype(jnp.bfloat16) for one in pick], axis=0
                )
                keys = kv[c, pl.ds(pl.multiple_of(start, side_rows), 2 * side_rows), pl.ds(base, window)]
                found = lax.dot_general(
                    both, keys, (((1,), (1,)), ((), ())), preferred_element_type=jnp.float32
                )
                stages.append((c, start, base, pick, found))
        weights = []
        for c, start, base, pick, found in stages:
            score = found * scale + bias[...]
            top = jnp.max(score, axis=-1, keepdims=True)
            expo = jnp.exp(score - top)
            total = jnp.sum(expo, axis=-1, keepdims=True)
            weights.append((expo * (1.0 / total)).astype(jnp.bfloat16))
        tiles = None
        for index, (c, start, base, pick, found) in enumerate(stages):
            if index % (HEADS // 2) == 0:
                tiles = [None] * (half // LANE)
            values = kv[
                c, pl.ds(pl.multiple_of(start, side_rows), 2 * side_rows), pl.ds(half + base, window)
            ]
            blend = jnp.dot(weights[index], values, preferred_element_type=jnp.float32)
            part = jnp.where(pick[0], blend[:side_rows], 0.0) + jnp.where(
                pick[1], blend[side_rows:], 0.0
            )
            for half_window in range(2):
                piece = part[:, half_window * LANE : (half_window + 1) * LANE]
                at = base // LANE + half_window
                tiles[at] = piece if tiles[at] is None else tiles[at] + piece
            if index % (HEADS // 2) == HEADS // 2 - 1:
                mixed = jnp.concatenate(tiles, axis=1).astype(jnp.bfloat16)
                mixed_out[c, aligned(start, side_rows), :] = mixed

    def give_far(c):
        for d in (2, 3):
            send_mix(d, c).start()

    def give_near(c):
        send_mix(1, c).start()
        mixed_in[0, c] = mixed_out[c, aligned(r * rows, rows), :]

    far_row = (1 - side) * side_rows

    def project_halo(c):
        for weight, lane in ((wk, 0), (wv, half)):
            part = jnp.dot(halo[c], weight[...], preferred_element_type=jnp.float32)
            kv[c, pl.ds(0, side_rows), pl.ds(lane, half)] = part.astype(jnp.bfloat16)

    @pl.when(high_side)
    def _():
        take(2, 0)

    take(3, 0)
    project(nrm[0, aligned(far_row, side_rows), :], 0, far_row, (side_rows, half))

    @pl.when(high_side & has_before)
    def _():
        wait_halo(0)
        project_halo(0)

    attend([(0, 1 - side)])
    give_far(0)
    take(2, 1)

    def chunk(c, carry):
        need = c - 1 + side
        take(3, c)

        @pl.when(has_before)
        def _():
            wait_halo(need)

        remote = nrm[c, aligned(far_row, side_rows), :]
        joined = jnp.concatenate([remote, halo[need]], axis=0)
        for weight, lane in ((wk, 0), (wv, half)):
            part = jnp.dot(joined, weight[...], preferred_element_type=jnp.float32)
            part = part.astype(jnp.bfloat16)
            kv[c, aligned(side_rows + far_row, side_rows), pl.ds(lane, half)] = part[:side_rows]

            @pl.when(has_before)
            def _():
                kv[need, pl.ds(0, side_rows), pl.ds(lane, half)] = part[side_rows:]

        query = jnp.dot(remote, wq[...], preferred_element_type=jnp.float32)
        qry[c, aligned(far_row, side_rows), :] = query.astype(jnp.bfloat16)
        attend([(c, 1 - side)])
        give_far(c)

        @pl.when(c + 1 < chunks)
        def _():
            take(2, c + 1)

        attend([(c - 1, side)])
        give_near(c - 1)
        return carry

    lax.fori_loop(1, chunks, chunk, 0)

    def finish(k, own):
        t = step_of(k, own)
        begin = 0 if own else 2
        taken = mixed_in[pl.ds(begin, 2), pl.ds(2 * k, 2)].reshape(2 * tub * TILE, half)
        result = jnp.dot(taken, wo[...], preferred_element_type=jnp.float32)
        result = result.reshape(2, 2, tub, SUB, width)
        for g in range(2):
            whole = jnp.concatenate([result[g, 0], result[g, 1]], axis=1)
            whole = whole + emb[t, g].astype(jnp.float32)
            target = peers[begin + g] * block + k * TILE
            encoded[:, aligned(target, TILE), :] = whole.astype(jnp.bfloat16)

    get_wo.wait()
    for c in range(2):
        send_mix(1, c).wait_recv()
    finish(0, True)

    @pl.when(low_side & has_before)
    def _():
        wait_halo(chunks - 1)
        project_halo(chunks - 1)

    attend([(chunks - 1, side)])
    give_near(chunks - 1)

    for c in range(2):
        for d in (2, 3):
            send_mix(d, c).wait_recv()
    finish(0, False)
    for c in range(2, 4):
        send_mix(1, c).wait_recv()
    finish(1, True)
    for c in range(2, 4):
        for d in (2, 3):
            send_mix(d, c).wait_recv()
    finish(1, False)

    def drain(c, carry):
        for d in range(1, QUAD):
            send_mix(d, c).wait_send()
        send_norm(1, c).wait_send()
        send_norm(3, c).wait_send()
        short = in_first & high_side & (c < 2)

        @pl.when(short)
        def _():
            send_rest(c).wait_send()

        @pl.when(jnp.logical_not(short))
        def _():
            send_norm(2, c).wait_send()

        @pl.when(has_after)
        def _():
            for g in range(2):
                halo_copy(nrm.at[c, pl.ds(0, rows)], g, c, 0, me + QUAD).wait_send()

        return carry

    lax.fori_loop(0, chunks, drain, 0)

    @pl.when(in_first & high_side)
    def _():
        send_raw().wait_send()


def body(pixels, prior_kv, w_embed, ln_gain, w_query, w_key, w_value, w_out):
    tub, pat, pix = pixels.shape
    width = w_embed.shape[1]
    half = w_key.shape[1]
    block = pat // QUAD
    chunks = block // SUB
    rows = tub * SUB
    bf16 = jnp.bfloat16
    dma = pltpu.SemaphoreType.DMA
    return pl.pallas_call(
        kernel,
        out_shape=pltpu.VMEM((tub, pat, width), bf16),
        in_specs=[pl.BlockSpec(memory_space=pl.ANY)] * 8,
        out_specs=pl.BlockSpec(memory_space=pltpu.VMEM),
        scratch_shapes=[
            pltpu.VMEM((4, 2, tub, TILE, pix), bf16),
            pltpu.VMEM((RAW, TILE, pix), bf16),
            pltpu.VMEM((2, 2 * tub, block, half), bf16),
            pltpu.VMEM(w_embed.shape, bf16),
            pltpu.VMEM((width,), jnp.float32),
            pltpu.VMEM(w_query.shape, bf16),
            pltpu.VMEM(w_key.shape, bf16),
            pltpu.VMEM(w_value.shape, bf16),
            pltpu.VMEM(w_out.shape, bf16),
            pltpu.VMEM((4, 2, tub, TILE, width), bf16),
            pltpu.VMEM((4, 2, 2, rows, width), bf16),
            pltpu.VMEM((chunks, QUAD * rows, width), bf16),
            pltpu.VMEM((chunks, 2 * rows, width), bf16),
            pltpu.VMEM((chunks, QUAD * rows, half), bf16),
            pltpu.VMEM((chunks, 6 * rows, 2 * half), bf16),
            pltpu.VMEM((chunks, QUAD * rows, half), bf16),
            pltpu.VMEM((QUAD, chunks, rows, half), bf16),
            pltpu.VMEM((QUAD * rows, QUAD * rows), jnp.float32),
            dma((6,)),
            dma((4, 2)),
            dma((1,)),
            dma((2,)),
            dma((QUAD, chunks)),
            dma((QUAD, chunks)),
            dma((2, chunks)),
            dma((2, chunks)),
            dma((QUAD, chunks)),
            dma((QUAD, chunks)),
        ],
        compiler_params=pltpu.CompilerParams(
            collective_id=0, has_side_effects=True, vmem_limit_bytes=60000000
        ),
    )(pixels, prior_kv, w_embed, ln_gain, w_query, w_key, w_value, w_out)


def solution(mesh):
    placed = (
        P(("groups", "tm"), None, None),
        P(None, "groups", None, None),
        P(),
        P(),
        P(),
        P(),
        P(),
        P(),
    )
    return jax.shard_map(
        body, mesh=mesh, in_specs=placed, out_specs=P(("groups", "tm"), None, None), check_vma=False
    )
```

```python
import math

import jax
import jax.numpy as jnp
from jax import lax
from jax.experimental import pallas as pl
from jax.experimental.pallas import tpu as pltpu
from jax.sharding import PartitionSpec as P

HEADS = 8
HEAD_DIM = 80
LANE = 128
TILE = 16
SUB = 8
RAW = 2
QUAD = 4
MESH = pl.DeviceIdType.MESH


def kernel(
    pixels,
    prior,
    w_embed,
    ln_gain,
    w_query,
    w_key,
    w_value,
    w_out,
    encoded,
    pix,
    raw,
    old,
    we,
    gain,
    wq,
    wk,
    wv,
    wo,
    emb,
    out_norm,
    nrm,
    halo,
    qry,
    kv,
    mixed_out,
    mixed_in,
    bias,
    w_sem,
    pix_sem,
    old_sem,
    raw_sem,
    norm_send,
    norm_recv,
    halo_send,
    halo_recv,
    mix_send,
    mix_recv,
):
    count = lax.axis_size("tm")
    me = lax.axis_index("tm")
    tub, patches, _ = pixels.shape
    width = w_embed.shape[1]
    half = w_key.shape[1]
    block = patches // QUAD
    chunks = block // SUB
    rows = tub * SUB
    side_rows = 2 * rows
    r = lax.rem(me, QUAD)
    first = me - r
    side = r // 2
    peers = [r, r + 1 - 2 * lax.rem(r, 2), lax.rem(r + 2, QUAD), QUAD - 1 - r]
    has_before = me >= QUAD
    has_after = me + QUAD < count
    low_side = side == 0
    in_first = me < QUAD
    high_side = side == 1

    def aligned(value, size):
        return pl.ds(pl.multiple_of(value, size), size)

    def step_of(k, own):
        return k + 1 if own else 3 * k

    def load_pix(t, g):
        own = t in (1, 2)
        source = peers[g if own else 2 + g] * block + (t // 2) * TILE
        return pltpu.make_async_copy(
            pixels.at[:, aligned(source, TILE), :], pix.at[t, g], pix_sem.at[t, g]
        )

    def wait_pix(t, g):
        pltpu.make_async_copy(
            pixels.at[:, pl.ds(0, TILE), :], pix.at[t, g], pix_sem.at[t, g]
        ).wait()

    def load_weight(source, target, index):
        return pltpu.make_async_copy(source, target, w_sem.at[index])

    get_we = load_weight(w_embed, we, 0)
    get_gain = load_weight(ln_gain, gain, 1)
    get_wk = load_weight(w_key, wk, 2)
    get_wv = load_weight(w_value, wv, 3)
    get_wq = load_weight(w_query, wq, 4)
    get_wo = load_weight(w_out, wo, 5)
    get_old = pltpu.make_async_copy(
        prior.at[:, :, aligned(r * block, block), :], old, old_sem.at[0]
    )

    def send_norm(d, c):
        k, h = c // 2, lax.rem(c, 2)
        t, g = (k + 1, 1) if d == 1 else (3 * k, d - 2)
        return pltpu.make_async_remote_copy(
            src_ref=out_norm.at[t, g, h],
            dst_ref=nrm.at[c, aligned(r * rows, rows)],
            send_sem=norm_send.at[d, c],
            recv_sem=norm_recv.at[d, c],
            device_id={"tm": first + peers[d]},
            device_id_type=MESH,
        )

    def send_raw():
        return pltpu.make_async_remote_copy(
            src_ref=pixels.at[pl.ds(0, RAW), aligned(peers[2] * block, TILE), :],
            dst_ref=raw,
            send_sem=raw_sem.at[0],
            recv_sem=raw_sem.at[1],
            device_id={"tm": first + peers[2]},
            device_id_type=MESH,
        )

    def send_rest(c):
        skip = RAW * SUB
        return pltpu.make_async_remote_copy(
            src_ref=out_norm.at[0, 0, c, pl.ds(skip, rows - skip)],
            dst_ref=nrm.at[c, pl.ds(pl.multiple_of(r * rows + skip, TILE), rows - skip)],
            send_sem=norm_send.at[2, c],
            recv_sem=norm_recv.at[2, c],
            device_id={"tm": first + peers[2]},
            device_id_type=MESH,
        )

    def halo_copy(source, g, c, j, target):
        return pltpu.make_async_remote_copy(
            src_ref=source,
            dst_ref=halo.at[c, aligned(j * rows, rows)],
            send_sem=halo_send.at[g, c],
            recv_sem=halo_recv.at[j, c],
            device_id={"tm": target},
            device_id_type=MESH,
        )

    def give_halo(t, g, h):
        c = 2 * (t // 2) + h
        return halo_copy(out_norm.at[t, g, h], g, c, lax.rem(r, 2), first + QUAD + peers[g])

    def forward_halo(d, c):
        source = nrm.at[c, aligned(peers[d] * rows, rows)]
        return halo_copy(source, d - 2, c, lax.rem(peers[d], 2), me + QUAD)

    def wait_halo(c):
        for j in range(2):
            halo_copy(nrm.at[c, pl.ds(0, rows)], 0, c, j, me + QUAD).wait_recv()

    def send_mix(d, c):
        return pltpu.make_async_remote_copy(
            src_ref=mixed_out.at[c, aligned(peers[d] * rows, rows)],
            dst_ref=mixed_in.at[d, c],
            send_sem=mix_send.at[d, c],
            recv_sem=mix_recv.at[d, c],
            device_id={"tm": first + peers[d]},
            device_id_type=MESH,
        )

    barrier = pltpu.get_barrier_semaphore()
    for d in range(1, QUAD):
        pl.semaphore_signal(
            barrier, inc=1, device_id={"tm": first + peers[d]}, device_id_type=MESH
        )

    def greet(target):
        pl.semaphore_signal(barrier, inc=1, device_id={"tm": target}, device_id_type=MESH)

    @pl.when(has_before)
    def _():
        greet(me - QUAD)

    @pl.when(has_after)
    def _():
        greet(me + QUAD)

    @pl.when(has_before & high_side)
    def _():
        greet(first - QUAD + peers[1])

    @pl.when(has_after & high_side)
    def _():
        greet(first + QUAD + peers[1])

    load_pix(0, 0).start()
    load_pix(0, 1).start()
    get_we.start()
    get_gain.start()

    def load_rest():
        for t in range(1, 4):
            for g in range(2):
                load_pix(t, g).start()
        get_wk.start()
        get_wv.start()
        get_wq.start()

        @pl.when(me < QUAD)
        def _():
            get_old.start()

        get_wo.start()

    row = lax.broadcasted_iota(jnp.int32, (2 * side_rows, 2 * side_rows), 0)
    col = lax.broadcasted_iota(jnp.int32, (2 * side_rows, 2 * side_rows), 1)
    at_t = lax.rem(row, side_rows) // SUB
    at_s = col // SUB
    seen = (lax.rem(row, SUB) == lax.rem(col, SUB)) & (at_s >= at_t) & (at_s <= at_t + 2 * tub)
    bias[...] = jnp.where(seen, 0.0, -jnp.inf)

    around = has_before.astype(jnp.int32) + has_after.astype(jnp.int32)
    pl.semaphore_wait(barrier, QUAD - 1 + around * (1 + side))

    @pl.when(in_first & high_side)
    def _():
        send_raw().start()

    def take(d, c):
        if d == 2:
            short = in_first & low_side & (c < 2)

            @pl.when(short)
            def _():
                send_rest(c).wait_recv()

            @pl.when(jnp.logical_not(short))
            def _():
                send_norm(2, c).wait_recv()

        else:
            send_norm(3, c).wait_recv()

        @pl.when(low_side & has_after)
        def _():
            forward_halo(d, c).start()

    def project(normed, cs, row0, shape):
        for weight, lane in ((wk, 0), (wv, half)):
            part = jnp.dot(normed, weight[...], preferred_element_type=jnp.float32)
            kv[cs, aligned(side_rows + row0, side_rows), pl.ds(lane, half)] = part.astype(
                jnp.bfloat16
            ).reshape(shape)
        query = jnp.dot(normed, wq[...], preferred_element_type=jnp.float32)
        qry[cs, aligned(row0, side_rows), :] = query.astype(jnp.bfloat16).reshape(shape)

    def normalize(flat):
        embedded = jnp.dot(flat, we[...], preferred_element_type=jnp.float32).astype(jnp.bfloat16)
        wide = embedded.astype(jnp.float32)
        center = wide - jnp.mean(wide, axis=-1, keepdims=True)
        spread = jnp.mean(center * center, axis=-1, keepdims=True)
        return embedded, center * lax.rsqrt(spread + 1e-06) * gain[...].reshape(1, width)

    def take_raw():
        send_raw().wait_recv()
        _, scaled = normalize(raw[...].reshape(RAW * TILE, pix.shape[4]))
        scaled = scaled.reshape(RAW, TILE, width)
        for h in range(2):
            piece = scaled[:, h * SUB : (h + 1) * SUB, :].reshape(RAW * SUB, width)
            start = pl.multiple_of(peers[2] * rows, rows)
            nrm[h, pl.ds(start, RAW * SUB), :] = piece.astype(jnp.bfloat16)

    def embed(t, carry):
        k = t // 2
        own = (t == 1) | (t == 2)
        for g in range(2):
            wait_pix(t, g)

        @pl.when(t == 0)
        def _():
            get_we.wait()
            get_gain.wait()
            load_rest()

        embedded, scaled = normalize(pix[t].reshape(2 * tub * TILE, pix.shape[4]))
        emb[t] = embedded.reshape(2, tub, TILE, width)
        scaled = scaled.reshape(2, tub, TILE, width)
        for g in range(2):
            for h in range(2):
                piece = scaled[g, :, h * SUB : (h + 1) * SUB, :].reshape(rows, width)
                out_norm[t, g, h] = piece.astype(jnp.bfloat16)

        @pl.when(own)
        def _():
            for h in range(2):
                send_norm(1, 2 * k + h).start()
                nrm[2 * k + h, aligned(r * rows, rows), :] = out_norm[t, 0, h]

            @pl.when(high_side & has_after)
            def _():
                for h in range(2):
                    for g in range(2):
                        give_halo(t, g, h).start()

        @pl.when(jnp.logical_not(own))
        def _():
            for h in range(2):
                short = in_first & high_side & (t == 0)

                @pl.when(short)
                def _():
                    send_rest(h).start()

                @pl.when(jnp.logical_not(short))
                def _():
                    send_norm(2, 2 * k + h).start()

                send_norm(3, 2 * k + h).start()

        return carry

    lax.fori_loop(0, 4, embed, 0)

    def project_local(k):
        for h in range(2):
            send_norm(1, 2 * k + h).wait_recv()
        cs = pl.ds(2 * k, 2)
        normed = nrm[cs, aligned(side * side_rows, side_rows), :]
        project(
            normed.reshape(2 * side_rows, width), cs, side * side_rows, (2, side_rows, half)
        )

    @pl.when(low_side)
    def _():
        @pl.when(in_first)
        def _():
            take_raw()

        take(2, 0)

    get_wk.wait()
    get_wv.wait()
    get_wq.wait()
    project_local(0)

    @pl.when(me < QUAD)
    def _():
        get_old.wait()
        for which in range(2):
            for k in range(chunks // 2):
                wide = old[which, :, k * TILE : (k + 1) * TILE, :].astype(jnp.float32)
                for h in range(2):
                    piece = wide[:, h * SUB : (h + 1) * SUB, :].reshape(side_rows, half)
                    kv[2 * k + h, pl.ds(0, side_rows), pl.ds(which * half, half)] = piece.astype(
                        jnp.bfloat16
                    )

    scale = 1.0 / math.sqrt(HEAD_DIM)
    window = 2 * LANE
    lane = lax.broadcasted_iota(jnp.int32, (1, window), 1)

    def attend(jobs):
        stages = []
        for c, which in jobs:
            start = which * side_rows
            for pair in range(HEADS // 2):
                low = 2 * pair * HEAD_DIM
                base = low // LANE * LANE
                begins = [low + head * HEAD_DIM - base for head in range(2)]
                pick = [(lane >= begin) & (lane < begin + HEAD_DIM) for begin in begins]
                q = qry[c, aligned(start, side_rows), pl.ds(base, window)]
                both = jnp.concatenate(
                    [q * jnp.where(one, 1.0, 0.0).astype(jnp.bfloat16) for one in pick], axis=0
                )
                keys = kv[c, pl.ds(pl.multiple_of(start, side_rows), 2 * side_rows), pl.ds(base, window)]
                found = lax.dot_general(
                    both, keys, (((1,), (1,)), ((), ())), preferred_element_type=jnp.float32
                )
                stages.append((c, start, base, pick, found))
        weights = []
        for c, start, base, pick, found in stages:
            score = found * scale + bias[...]
            top = jnp.max(score, axis=-1, keepdims=True)
            expo = jnp.exp(score - top)
            total = jnp.sum(expo, axis=-1, keepdims=True)
            weights.append((expo * (1.0 / total)).astype(jnp.bfloat16))
        tiles = None
        for index, (c, start, base, pick, found) in enumerate(stages):
            if index % (HEADS // 2) == 0:
                tiles = [None] * (half // LANE)
            values = kv[
                c, pl.ds(pl.multiple_of(start, side_rows), 2 * side_rows), pl.ds(half + base, window)
            ]
            blend = jnp.dot(weights[index], values, preferred_element_type=jnp.float32)
            part = jnp.where(pick[0], blend[:side_rows], 0.0) + jnp.where(
                pick[1], blend[side_rows:], 0.0
            )
            for half_window in range(2):
                piece = part[:, half_window * LANE : (half_window + 1) * LANE]
                at = base // LANE + half_window
                tiles[at] = piece if tiles[at] is None else tiles[at] + piece
            if index % (HEADS // 2) == HEADS // 2 - 1:
                mixed = jnp.concatenate(tiles, axis=1).astype(jnp.bfloat16)
                mixed_out[c, aligned(start, side_rows), :] = mixed

    def give_far(c):
        for d in (2, 3):
            send_mix(d, c).start()

    def give_near(c):
        send_mix(1, c).start()
        mixed_in[0, c] = mixed_out[c, aligned(r * rows, rows), :]

    far_row = (1 - side) * side_rows

    def project_halo(c):
        for weight, lane in ((wk, 0), (wv, half)):
            part = jnp.dot(halo[c], weight[...], preferred_element_type=jnp.float32)
            kv[c, pl.ds(0, side_rows), pl.ds(lane, half)] = part.astype(jnp.bfloat16)

    @pl.when(high_side)
    def _():
        take(2, 0)

    take(3, 0)
    project(nrm[0, aligned(far_row, side_rows), :], 0, far_row, (side_rows, half))

    @pl.when(high_side & has_before)
    def _():
        wait_halo(0)
        project_halo(0)

    attend([(0, 1 - side)])
    give_far(0)
    take(2, 1)
    project_local(1)

    def chunk(c, carry):
        need = c - 1 + side
        take(3, c)

        @pl.when(has_before)
        def _():
            wait_halo(need)

        remote = nrm[c, aligned(far_row, side_rows), :]
        joined = jnp.concatenate([remote, halo[need]], axis=0)
        for weight, lane in ((wk, 0), (wv, half)):
            part = jnp.dot(joined, weight[...], preferred_element_type=jnp.float32)
            part = part.astype(jnp.bfloat16)
            kv[c, aligned(side_rows + far_row, side_rows), pl.ds(lane, half)] = part[:side_rows]

            @pl.when(has_before)
            def _():
                kv[need, pl.ds(0, side_rows), pl.ds(lane, half)] = part[side_rows:]

        query = jnp.dot(remote, wq[...], preferred_element_type=jnp.float32)
        qry[c, aligned(far_row, side_rows), :] = query.astype(jnp.bfloat16)
        attend([(c, 1 - side)])
        give_far(c)

        @pl.when(c + 1 < chunks)
        def _():
            take(2, c + 1)

        attend([(c - 1, side)])
        give_near(c - 1)
        return carry

    lax.fori_loop(1, chunks, chunk, 0)

    def finish(k, own):
        t = step_of(k, own)
        begin = 0 if own else 2
        taken = mixed_in[pl.ds(begin, 2), pl.ds(2 * k, 2)].reshape(2 * tub * TILE, half)
        result = jnp.dot(taken, wo[...], preferred_element_type=jnp.float32)
        result = result.reshape(2, 2, tub, SUB, width)
        for g in range(2):
            whole = jnp.concatenate([result[g, 0], result[g, 1]], axis=1)
            whole = whole + emb[t, g].astype(jnp.float32)
            target = peers[begin + g] * block + k * TILE
            encoded[:, aligned(target, TILE), :] = whole.astype(jnp.bfloat16)

    get_wo.wait()
    for c in range(2):
        send_mix(1, c).wait_recv()
    finish(0, True)
    def drain_rows(c, carry):
        send_norm(1, c).wait_send()
        send_norm(3, c).wait_send()
        short = in_first & high_side & (c < 2)

        @pl.when(short)
        def _():
            send_rest(c).wait_send()

        @pl.when(jnp.logical_not(short))
        def _():
            send_norm(2, c).wait_send()

        @pl.when(has_after)
        def _():
            for g in range(2):
                halo_copy(nrm.at[c, pl.ds(0, rows)], g, c, 0, me + QUAD).wait_send()

        return carry

    lax.fori_loop(0, chunks, drain_rows, 0)

    @pl.when(in_first & high_side)
    def _():
        send_raw().wait_send()


    @pl.when(low_side & has_before)
    def _():
        wait_halo(chunks - 1)
        project_halo(chunks - 1)

    attend([(chunks - 1, side)])
    give_near(chunks - 1)

    for c in range(2):
        for d in (2, 3):
            send_mix(d, c).wait_recv()
    finish(0, False)
    for c in range(2, 4):
        send_mix(1, c).wait_recv()
    finish(1, True)
    def drain_mix(c, carry):
        for d in range(1, QUAD):
            send_mix(d, c).wait_send()
        return carry

    lax.fori_loop(0, chunks - 1, drain_mix, 0)
    send_mix(1, chunks - 1).wait_send()
    for c in range(2, 4):
        for d in (2, 3):
            send_mix(d, c).wait_recv()
    finish(1, False)

    for d in (2, 3):
        send_mix(d, chunks - 1).wait_send()


def body(pixels, prior_kv, w_embed, ln_gain, w_query, w_key, w_value, w_out):
    tub, pat, pix = pixels.shape
    width = w_embed.shape[1]
    half = w_key.shape[1]
    block = pat // QUAD
    chunks = block // SUB
    rows = tub * SUB
    bf16 = jnp.bfloat16
    dma = pltpu.SemaphoreType.DMA
    return pl.pallas_call(
        kernel,
        out_shape=pltpu.VMEM((tub, pat, width), bf16),
        in_specs=[pl.BlockSpec(memory_space=pl.ANY)] * 8,
        out_specs=pl.BlockSpec(memory_space=pltpu.VMEM),
        scratch_shapes=[
            pltpu.VMEM((4, 2, tub, TILE, pix), bf16),
            pltpu.VMEM((RAW, TILE, pix), bf16),
            pltpu.VMEM((2, 2 * tub, block, half), bf16),
            pltpu.VMEM(w_embed.shape, bf16),
            pltpu.VMEM((width,), jnp.float32),
            pltpu.VMEM(w_query.shape, bf16),
            pltpu.VMEM(w_key.shape, bf16),
            pltpu.VMEM(w_value.shape, bf16),
            pltpu.VMEM(w_out.shape, bf16),
            pltpu.VMEM((4, 2, tub, TILE, width), bf16),
            pltpu.VMEM((4, 2, 2, rows, width), bf16),
            pltpu.VMEM((chunks, QUAD * rows, width), bf16),
            pltpu.VMEM((chunks, 2 * rows, width), bf16),
            pltpu.VMEM((chunks, QUAD * rows, half), bf16),
            pltpu.VMEM((chunks, 6 * rows, 2 * half), bf16),
            pltpu.VMEM((chunks, QUAD * rows, half), bf16),
            pltpu.VMEM((QUAD, chunks, rows, half), bf16),
            pltpu.VMEM((QUAD * rows, QUAD * rows), jnp.float32),
            dma((6,)),
            dma((4, 2)),
            dma((1,)),
            dma((2,)),
            dma((QUAD, chunks)),
            dma((QUAD, chunks)),
            dma((2, chunks)),
            dma((2, chunks)),
            dma((QUAD, chunks)),
            dma((QUAD, chunks)),
        ],
        compiler_params=pltpu.CompilerParams(
            collective_id=0, has_side_effects=True, vmem_limit_bytes=60000000
        ),
    )(pixels, prior_kv, w_embed, ln_gain, w_query, w_key, w_value, w_out)


def solution(mesh):
    placed = (
        P(("groups", "tm"), None, None),
        P(None, "groups", None, None),
        P(),
        P(),
        P(),
        P(),
        P(),
        P(),
    )
    return jax.shard_map(
        body, mesh=mesh, in_specs=placed, out_specs=P(("groups", "tm"), None, None), check_vma=False
    )
```

```python
import math

import jax
import jax.numpy as jnp
from jax import lax
from jax.experimental import pallas as pl
from jax.experimental.pallas import tpu as pltpu
from jax.sharding import PartitionSpec as P

HEADS = 8
HEAD_DIM = 80
LANE = 128
TILE = 16
SUB = 8
RAW = 2
QUAD = 4
MESH = pl.DeviceIdType.MESH


def kernel(
    pixels,
    prior,
    w_embed,
    ln_gain,
    w_query,
    w_key,
    w_value,
    w_out,
    encoded,
    pix,
    raw,
    old,
    old_far,
    we,
    gain,
    wq,
    wk,
    wv,
    wo,
    emb,
    out_norm,
    nrm,
    halo,
    extra,
    qry,
    kv,
    mixed_out,
    mixed_in,
    bias,
    w_sem,
    pix_sem,
    old_sem,
    raw_sem,
    extra_sem,
    norm_send,
    norm_recv,
    halo_send,
    halo_recv,
    mix_send,
    mix_recv,
):
    count = lax.axis_size("tm")
    me = lax.axis_index("tm")
    tub, patches, _ = pixels.shape
    width = w_embed.shape[1]
    half = w_key.shape[1]
    block = patches // QUAD
    chunks = block // SUB
    rows = tub * SUB
    side_rows = 2 * rows
    r = lax.rem(me, QUAD)
    first = me - r
    side = r // 2
    peers = [r, r + 1 - 2 * lax.rem(r, 2), lax.rem(r + 2, QUAD), QUAD - 1 - r]
    has_before = me >= QUAD
    has_after = me + QUAD < count
    low_side = side == 0
    in_first = me < QUAD
    local_far = in_first & low_side
    high_side = side == 1

    def aligned(value, size):
        return pl.ds(pl.multiple_of(value, size), size)

    def step_of(k, own):
        return k + 1 if own else 3 * k

    def load_pix(t, g):
        own = t in (1, 2)
        source = peers[g if own else 2 + g] * block + (t // 2) * TILE
        return pltpu.make_async_copy(
            pixels.at[:, aligned(source, TILE), :], pix.at[t, g], pix_sem.at[t, g]
        )

    def wait_pix(t, g):
        pltpu.make_async_copy(
            pixels.at[:, pl.ds(0, TILE), :], pix.at[t, g], pix_sem.at[t, g]
        ).wait()

    def load_weight(source, target, index):
        return pltpu.make_async_copy(source, target, w_sem.at[index])

    get_we = load_weight(w_embed, we, 0)
    get_gain = load_weight(ln_gain, gain, 1)
    get_wk = load_weight(w_key, wk, 2)
    get_wv = load_weight(w_value, wv, 3)
    get_wq = load_weight(w_query, wq, 4)
    get_wo = load_weight(w_out, wo, 5)
    get_old = pltpu.make_async_copy(
        prior.at[:, :, aligned(r * block, block), :], old, old_sem.at[0]
    )

    get_old_far = pltpu.make_async_copy(
        prior.at[:, :, aligned(peers[2] * block + block - TILE, TILE), :], old_far, old_sem.at[1]
    )

    def send_norm(d, c):
        k, h = c // 2, lax.rem(c, 2)
        t, g = (k + 1, 1) if d == 1 else (3 * k, d - 2)
        return pltpu.make_async_remote_copy(
            src_ref=out_norm.at[t, g, h],
            dst_ref=nrm.at[c, aligned(r * rows, rows)],
            send_sem=norm_send.at[d, c],
            recv_sem=norm_recv.at[d, c],
            device_id={"tm": first + peers[d]},
            device_id_type=MESH,
        )

    def send_raw():
        return pltpu.make_async_remote_copy(
            src_ref=pixels.at[pl.ds(0, RAW), aligned(peers[2] * block, TILE), :],
            dst_ref=raw,
            send_sem=raw_sem.at[0],
            recv_sem=raw_sem.at[1],
            device_id={"tm": first + peers[2]},
            device_id_type=MESH,
        )

    def send_rest(c):
        skip = RAW * SUB
        return pltpu.make_async_remote_copy(
            src_ref=out_norm.at[0, 0, c, pl.ds(skip, rows - skip)],
            dst_ref=nrm.at[c, pl.ds(pl.multiple_of(r * rows + skip, TILE), rows - skip)],
            send_sem=norm_send.at[2, c],
            recv_sem=norm_recv.at[2, c],
            device_id={"tm": first + peers[2]},
            device_id_type=MESH,
        )

    def send_extra():
        return pltpu.make_async_remote_copy(
            src_ref=out_norm.at[3, 1, 1],
            dst_ref=extra.at[aligned(r * rows, rows)],
            send_sem=extra_sem.at[0],
            recv_sem=extra_sem.at[1],
            device_id={"tm": first + peers[1]},
            device_id_type=MESH,
        )

    def return_extra():
        return pltpu.make_async_remote_copy(
            src_ref=mixed_out.at[chunks, aligned(peers[1] * rows, rows)],
            dst_ref=mixed_in.at[3, chunks - 1],
            send_sem=extra_sem.at[2],
            recv_sem=mix_recv.at[3, chunks - 1],
            device_id={"tm": first + peers[1]},
            device_id_type=MESH,
        )

    def halo_copy(source, g, c, j, target):
        return pltpu.make_async_remote_copy(
            src_ref=source,
            dst_ref=halo.at[c, aligned(j * rows, rows)],
            send_sem=halo_send.at[g, c],
            recv_sem=halo_recv.at[j, c],
            device_id={"tm": target},
            device_id_type=MESH,
        )

    def give_halo(t, g, h):
        c = 2 * (t // 2) + h
        return halo_copy(out_norm.at[t, g, h], g, c, lax.rem(r, 2), first + QUAD + peers[g])

    def forward_halo(d, c):
        source = nrm.at[c, aligned(peers[d] * rows, rows)]
        return halo_copy(source, d - 2, c, lax.rem(peers[d], 2), me + QUAD)

    def wait_halo(c):
        for j in range(2):
            halo_copy(nrm.at[c, pl.ds(0, rows)], 0, c, j, me + QUAD).wait_recv()

    def send_mix(d, c):
        return pltpu.make_async_remote_copy(
            src_ref=mixed_out.at[c, aligned(peers[d] * rows, rows)],
            dst_ref=mixed_in.at[d, c],
            send_sem=mix_send.at[d, c],
            recv_sem=mix_recv.at[d, c],
            device_id={"tm": first + peers[d]},
            device_id_type=MESH,
        )

    barrier = pltpu.get_barrier_semaphore()
    def greet(target):
        pl.semaphore_signal(barrier, inc=1, device_id={"tm": target}, device_id_type=MESH)

    @pl.when(has_before)
    def _():
        greet(me - QUAD)

    @pl.when(has_after)
    def _():
        greet(me + QUAD)

    @pl.when(has_before & high_side)
    def _():
        greet(first - QUAD + peers[1])

    @pl.when(has_after & high_side)
    def _():
        greet(first + QUAD + peers[1])

    for d in range(1, QUAD):
        greet(first + peers[d])

    load_pix(0, 0).start()
    load_pix(0, 1).start()
    get_we.start()
    get_gain.start()

    def load_rest():
        for t in range(1, 4):
            for g in range(2):
                load_pix(t, g).start()
        get_wk.start()
        get_wv.start()
        get_wq.start()

        @pl.when(me < QUAD)
        def _():
            get_old.start()

        @pl.when(local_far)
        def _():
            get_old_far.start()

        get_wo.start()

    row = lax.broadcasted_iota(jnp.int32, (2 * side_rows, 2 * side_rows), 0)
    col = lax.broadcasted_iota(jnp.int32, (2 * side_rows, 2 * side_rows), 1)
    at_t = lax.rem(row, side_rows) // SUB
    at_s = col // SUB
    seen = (lax.rem(row, SUB) == lax.rem(col, SUB)) & (at_s >= at_t) & (at_s <= at_t + 2 * tub)
    bias[...] = jnp.where(seen, 0.0, -jnp.inf)

    around = has_before.astype(jnp.int32) + has_after.astype(jnp.int32)
    pl.semaphore_wait(barrier, QUAD - 1 + around * (1 + side))

    @pl.when(in_first & high_side)
    def _():
        send_raw().start()

    def take(d, c):
        if d == 2:
            short = in_first & low_side & (c < 2)

            @pl.when(short)
            def _():
                send_rest(c).wait_recv()

            @pl.when(jnp.logical_not(short))
            def _():
                send_norm(2, c).wait_recv()

        else:
            send_norm(3, c).wait_recv()

        @pl.when(low_side & has_after)
        def _():
            forward_halo(d, c).start()

    def project(normed, cs, row0, shape):
        for weight, lane in ((wk, 0), (wv, half)):
            part = jnp.dot(normed, weight[...], preferred_element_type=jnp.float32)
            kv[cs, aligned(side_rows + row0, side_rows), pl.ds(lane, half)] = part.astype(
                jnp.bfloat16
            ).reshape(shape)
        query = jnp.dot(normed, wq[...], preferred_element_type=jnp.float32)
        qry[cs, aligned(row0, side_rows), :] = query.astype(jnp.bfloat16).reshape(shape)

    def normalize(flat):
        embedded = jnp.dot(flat, we[...], preferred_element_type=jnp.float32).astype(jnp.bfloat16)
        wide = embedded.astype(jnp.float32)
        center = wide - jnp.mean(wide, axis=-1, keepdims=True)
        spread = jnp.mean(center * center, axis=-1, keepdims=True)
        return embedded, center * lax.rsqrt(spread + 1e-06) * gain[...].reshape(1, width)

    def take_raw():
        send_raw().wait_recv()
        _, scaled = normalize(raw[...].reshape(RAW * TILE, pix.shape[4]))
        scaled = scaled.reshape(RAW, TILE, width)
        for h in range(2):
            piece = scaled[:, h * SUB : (h + 1) * SUB, :].reshape(RAW * SUB, width)
            start = pl.multiple_of(peers[2] * rows, rows)
            nrm[h, pl.ds(start, RAW * SUB), :] = piece.astype(jnp.bfloat16)

    def embed(t, carry):
        k = t // 2
        own = (t == 1) | (t == 2)
        for g in range(2):
            wait_pix(t, g)

        @pl.when(t == 0)
        def _():
            get_we.wait()
            get_gain.wait()
            load_rest()

        embedded, scaled = normalize(pix[t].reshape(2 * tub * TILE, pix.shape[4]))
        emb[t] = embedded.reshape(2, tub, TILE, width)
        scaled = scaled.reshape(2, tub, TILE, width)
        for g in range(2):
            for h in range(2):
                piece = scaled[g, :, h * SUB : (h + 1) * SUB, :].reshape(rows, width)
                out_norm[t, g, h] = piece.astype(jnp.bfloat16)

        @pl.when(own)
        def _():
            for h in range(2):
                send_norm(1, 2 * k + h).start()
                nrm[2 * k + h, aligned(r * rows, rows), :] = out_norm[t, 0, h]

            @pl.when(high_side & has_after)
            def _():
                for h in range(2):
                    for g in range(2):
                        give_halo(t, g, h).start()

        @pl.when(jnp.logical_not(own))
        def _():
            for h in range(2):
                short = in_first & high_side & (t == 0)

                @pl.when(short)
                def _():
                    send_rest(h).start()

                @pl.when(jnp.logical_not(short))
                def _():
                    send_norm(2, 2 * k + h).start()

                send_norm(3, 2 * k + h).start()

            @pl.when(local_far & (t == 3))
            def _():
                send_extra().start()
                extra[aligned(r * rows, rows), :] = out_norm[3, 0, 1]

        return carry

    lax.fori_loop(0, 4, embed, 0)

    def project_local(k):
        for h in range(2):
            send_norm(1, 2 * k + h).wait_recv()
        cs = pl.ds(2 * k, 2)
        normed = nrm[cs, aligned(side * side_rows, side_rows), :]
        project(
            normed.reshape(2 * side_rows, width), cs, side * side_rows, (2, side_rows, half)
        )

    @pl.when(low_side)
    def _():
        @pl.when(in_first)
        def _():
            take_raw()

        take(2, 0)

    get_wk.wait()
    get_wv.wait()
    get_wq.wait()
    project_local(0)

    @pl.when(me < QUAD)
    def _():
        get_old.wait()
        for which in range(2):
            for k in range(chunks // 2):
                wide = old[which, :, k * TILE : (k + 1) * TILE, :].astype(jnp.float32)
                for h in range(2):
                    piece = wide[:, h * SUB : (h + 1) * SUB, :].reshape(side_rows, half)
                    kv[2 * k + h, pl.ds(0, side_rows), pl.ds(which * half, half)] = piece.astype(
                        jnp.bfloat16
                    )

    scale = 1.0 / math.sqrt(HEAD_DIM)
    window = 2 * LANE
    lane = lax.broadcasted_iota(jnp.int32, (1, window), 1)

    def attend(jobs):
        stages = []
        for c, which in jobs:
            start = which * side_rows
            for pair in range(HEADS // 2):
                low = 2 * pair * HEAD_DIM
                base = low // LANE * LANE
                begins = [low + head * HEAD_DIM - base for head in range(2)]
                pick = [(lane >= begin) & (lane < begin + HEAD_DIM) for begin in begins]
                q = qry[c, aligned(start, side_rows), pl.ds(base, window)]
                both = jnp.concatenate(
                    [q * jnp.where(one, 1.0, 0.0).astype(jnp.bfloat16) for one in pick], axis=0
                )
                keys = kv[c, pl.ds(pl.multiple_of(start, side_rows), 2 * side_rows), pl.ds(base, window)]
                found = lax.dot_general(
                    both, keys, (((1,), (1,)), ((), ())), preferred_element_type=jnp.float32
                )
                stages.append((c, start, base, pick, found))
        weights = []
        for c, start, base, pick, found in stages:
            score = found * scale + bias[...]
            top = jnp.max(score, axis=-1, keepdims=True)
            expo = jnp.exp(score - top)
            total = jnp.sum(expo, axis=-1, keepdims=True)
            weights.append((expo * (1.0 / total)).astype(jnp.bfloat16))
        tiles = None
        for index, (c, start, base, pick, found) in enumerate(stages):
            if index % (HEADS // 2) == 0:
                tiles = [None] * (half // LANE)
            values = kv[
                c, pl.ds(pl.multiple_of(start, side_rows), 2 * side_rows), pl.ds(half + base, window)
            ]
            blend = jnp.dot(weights[index], values, preferred_element_type=jnp.float32)
            part = jnp.where(pick[0], blend[:side_rows], 0.0) + jnp.where(
                pick[1], blend[side_rows:], 0.0
            )
            for half_window in range(2):
                piece = part[:, half_window * LANE : (half_window + 1) * LANE]
                at = base // LANE + half_window
                tiles[at] = piece if tiles[at] is None else tiles[at] + piece
            if index % (HEADS // 2) == HEADS // 2 - 1:
                mixed = jnp.concatenate(tiles, axis=1).astype(jnp.bfloat16)
                mixed_out[c, aligned(start, side_rows), :] = mixed

    def give_far(c):
        for d in (2, 3):
            send_mix(d, c).start()

    def give_near(c):
        send_mix(1, c).start()
        mixed_in[0, c] = mixed_out[c, aligned(r * rows, rows), :]

    far_row = (1 - side) * side_rows

    def project_halo(c):
        for weight, lane in ((wk, 0), (wv, half)):
            part = jnp.dot(halo[c], weight[...], preferred_element_type=jnp.float32)
            kv[c, pl.ds(0, side_rows), pl.ds(lane, half)] = part.astype(jnp.bfloat16)

    @pl.when(high_side)
    def _():
        take(2, 0)

    take(3, 0)
    project(nrm[0, aligned(far_row, side_rows), :], 0, far_row, (side_rows, half))

    @pl.when(high_side & has_before)
    def _():
        wait_halo(0)
        project_halo(0)

    attend([(0, 1 - side)])
    give_far(0)
    take(2, 1)
    project_local(1)

    @pl.when(local_far)
    def _():
        get_old_far.wait()
        send_extra().wait_recv()
        for which in range(2):
            piece = old_far[which].astype(jnp.float32)[:, SUB:, :].reshape(side_rows, half)
            kv[chunks, pl.ds(0, side_rows), pl.ds(which * half, half)] = piece.astype(jnp.bfloat16)
        for weight, lane in ((wk, 0), (wv, half)):
            part = jnp.dot(extra[...], weight[...], preferred_element_type=jnp.float32)
            kv[chunks, pl.ds(side_rows, side_rows), pl.ds(lane, half)] = part.astype(jnp.bfloat16)
        query = jnp.dot(extra[...], wq[...], preferred_element_type=jnp.float32)
        qry[chunks, pl.ds(0, side_rows), :] = query.astype(jnp.bfloat16)

    def chunk(c, carry):
        need = c - 1 + side
        take(3, c)

        @pl.when(has_before)
        def _():
            wait_halo(need)

        remote = nrm[c, aligned(far_row, side_rows), :]
        joined = jnp.concatenate([remote, halo[need]], axis=0)
        for weight, lane in ((wk, 0), (wv, half)):
            part = jnp.dot(joined, weight[...], preferred_element_type=jnp.float32)
            part = part.astype(jnp.bfloat16)
            kv[c, aligned(side_rows + far_row, side_rows), pl.ds(lane, half)] = part[:side_rows]

            @pl.when(has_before)
            def _():
                kv[need, pl.ds(0, side_rows), pl.ds(lane, half)] = part[side_rows:]

        query = jnp.dot(remote, wq[...], preferred_element_type=jnp.float32)
        qry[c, aligned(far_row, side_rows), :] = query.astype(jnp.bfloat16)
        attend([(c, 1 - side)])

        @pl.when(jnp.logical_not(in_first & high_side & (c == chunks - 1)))
        def _():
            give_far(c)

        @pl.when(c + 1 < chunks)
        def _():
            take(2, c + 1)

        attend([(c - 1, side)])
        give_near(c - 1)
        return carry

    lax.fori_loop(1, chunks, chunk, 0)

    def finish(k, own):
        t = step_of(k, own)
        begin = 0 if own else 2
        taken = mixed_in[pl.ds(begin, 2), pl.ds(2 * k, 2)].reshape(2 * tub * TILE, half)
        result = jnp.dot(taken, wo[...], preferred_element_type=jnp.float32)
        result = result.reshape(2, 2, tub, SUB, width)
        for g in range(2):
            whole = jnp.concatenate([result[g, 0], result[g, 1]], axis=1)
            whole = whole + emb[t, g].astype(jnp.float32)
            target = peers[begin + g] * block + k * TILE
            encoded[:, aligned(target, TILE), :] = whole.astype(jnp.bfloat16)

    @pl.when(local_far)
    def _():
        attend([(chunks, 0)])
        return_extra().start()
        mixed_in[2, chunks - 1] = mixed_out[chunks, aligned(r * rows, rows)]

    get_wo.wait()
    for c in range(2):
        send_mix(1, c).wait_recv()
    finish(0, True)

    def drain_rows(c, carry):
        send_norm(1, c).wait_send()
        send_norm(3, c).wait_send()
        short = in_first & high_side & (c < 2)

        @pl.when(short)
        def _():
            send_rest(c).wait_send()

        @pl.when(jnp.logical_not(short))
        def _():
            send_norm(2, c).wait_send()

        @pl.when(has_after)
        def _():
            for g in range(2):
                halo_copy(nrm.at[c, pl.ds(0, rows)], g, c, 0, me + QUAD).wait_send()

        return carry

    lax.fori_loop(0, chunks, drain_rows, 0)

    @pl.when(in_first & high_side)
    def _():
        send_raw().wait_send()


    @pl.when(low_side & has_before)
    def _():
        wait_halo(chunks - 1)

    for weight, offset in ((wk, 0), (wv, half)):
        part = jnp.dot(halo[chunks - 1], weight[...], preferred_element_type=jnp.float32)
        place = (chunks - 1, pl.ds(0, side_rows), pl.ds(offset, half))
        kv[place] = jnp.where(has_before, part.astype(jnp.bfloat16), kv[place])

    attend([(chunks - 1, side)])
    give_near(chunks - 1)

    for c in range(2):
        for d in (2, 3):
            send_mix(d, c).wait_recv()
    finish(0, False)
    for c in range(2, 4):
        send_mix(1, c).wait_recv()
    finish(1, True)
    def drain_mix(c, carry):
        for d in range(1, QUAD):
            send_mix(d, c).wait_send()
        return carry

    lax.fori_loop(0, chunks - 1, drain_mix, 0)
    send_mix(1, chunks - 1).wait_send()
    for d in (2, 3):
        send_mix(d, 2).wait_recv()

    @pl.when(jnp.logical_not(local_far))
    def _():
        for d in (2, 3):
            send_mix(d, chunks - 1).wait_recv()

    @pl.when(local_far)
    def _():
        return_extra().wait_recv()

    finish(1, False)


    @pl.when(jnp.logical_not(in_first & high_side))
    def _():
        for d in (2, 3):
            send_mix(d, chunks - 1).wait_send()

    @pl.when(local_far)
    def _():
        send_extra().wait_send()
        return_extra().wait_send()


def body(pixels, prior_kv, w_embed, ln_gain, w_query, w_key, w_value, w_out):
    tub, pat, pix = pixels.shape
    width = w_embed.shape[1]
    half = w_key.shape[1]
    block = pat // QUAD
    chunks = block // SUB
    rows = tub * SUB
    bf16 = jnp.bfloat16
    dma = pltpu.SemaphoreType.DMA
    return pl.pallas_call(
        kernel,
        out_shape=pltpu.VMEM((tub, pat, width), bf16),
        in_specs=[pl.BlockSpec(memory_space=pl.ANY)] * 8,
        out_specs=pl.BlockSpec(memory_space=pltpu.VMEM),
        scratch_shapes=[
            pltpu.VMEM((4, 2, tub, TILE, pix), bf16),
            pltpu.VMEM((RAW, TILE, pix), bf16),
            pltpu.VMEM((2, 2 * tub, block, half), bf16),
            pltpu.VMEM((2, 2 * tub, TILE, half), bf16),
            pltpu.VMEM(w_embed.shape, bf16),
            pltpu.VMEM((width,), jnp.float32),
            pltpu.VMEM(w_query.shape, bf16),
            pltpu.VMEM(w_key.shape, bf16),
            pltpu.VMEM(w_value.shape, bf16),
            pltpu.VMEM(w_out.shape, bf16),
            pltpu.VMEM((4, 2, tub, TILE, width), bf16),
            pltpu.VMEM((4, 2, 2, rows, width), bf16),
            pltpu.VMEM((chunks, QUAD * rows, width), bf16),
            pltpu.VMEM((chunks, 2 * rows, width), bf16),
            pltpu.VMEM((2 * rows, width), bf16),
            pltpu.VMEM((chunks + 1, QUAD * rows, half), bf16),
            pltpu.VMEM((chunks + 1, 6 * rows, 2 * half), bf16),
            pltpu.VMEM((chunks + 1, QUAD * rows, half), bf16),
            pltpu.VMEM((QUAD, chunks, rows, half), bf16),
            pltpu.VMEM((QUAD * rows, QUAD * rows), jnp.float32),
            dma((6,)),
            dma((4, 2)),
            dma((2,)),
            dma((2,)),
            dma((3,)),
            dma((QUAD, chunks)),
            dma((QUAD, chunks)),
            dma((2, chunks)),
            dma((2, chunks)),
            dma((QUAD, chunks)),
            dma((QUAD, chunks)),
        ],
        compiler_params=pltpu.CompilerParams(
            collective_id=0, has_side_effects=True, vmem_limit_bytes=60000000
        ),
    )(pixels, prior_kv, w_embed, ln_gain, w_query, w_key, w_value, w_out)


def solution(mesh):
    placed = (
        P(("groups", "tm"), None, None),
        P(None, "groups", None, None),
        P(),
        P(),
        P(),
        P(),
        P(),
        P(),
    )
    return jax.shard_map(
        body, mesh=mesh, in_specs=placed, out_specs=P(("groups", "tm"), None, None), check_vma=False
    )
```
